512 devices in a mesh: along: 32 (over y, x, z_hi), cross: 16 (over z_lo, core).
Axes of the slice: x: 4, y: 4, z: 16 (z_hi: 2, z_lo: 8; z = z_hi * 8 + z_lo), core: 2. Of those that a mesh axis runs over, the one named last changes fastest.
Arguments:
- nadir_view: bfloat16 [8192, 24576], P('along', 'cross'), may hold values from -36 to 36
- forward: bfloat16 [8192, 24576], P('along', 'cross'), may hold values from -36 to 36
- backward: bfloat16 [8192, 24576], P('along', 'cross'), may hold values from -36 to 36
- along_weights: bfloat16 [2, 4, 8192], replicated, may hold values from 0.049804688 to 0.5
- cross_weights: bfloat16 [2, 4, 24576], P(None, None, 'cross'), may hold values from 0.049804688 to 0.5
- band_offsets: int32 [2, 8192], replicated, may hold values from -6 to 6, as said below
- col_offsets: int32 [2, 24576], P(None, 'cross'), may hold values from -6 to 6, as said below
- lag_lines: int32 [8192], replicated, may hold values from 20480 to 20495, as said below
- window_start: int32 [1], replicated, may hold values from 0 to 2088960
Outputs:
- parallax: bfloat16 [2, 8192, 24576], P(None, 'along', 'cross')
- normal_gram: float32 [32, 256, 256], P('along', 'cross')
- normal_rhs: float32 [32, 256], P('along', 'cross')
The draws below stay inside these ranges and needn't reach their ends.
Inputs may be any that keep to these rules, and one draw needn't show every extreme that they name: `lag_lines`: every value in the range occurs in each draw. `band_offsets`: both ends of the range occur in each draw. `col_offsets`: both ends of the range occur in each draw.
All inputs are finite; a program needn't handle non-finite values.
Results may differ from the reference program's by a relative error of at most 0.0065.
Values may be sent and summed in bfloat16 or wider, within the bound.
A program may use at most 64 MiB of HBM per device.

```python
import jax
import jax.numpy as jnp
from jax import lax

LD = 256
TAPS = 4
OFFA = 6
OFFC = 6
LAG_SPAN = 16
BOX = 4
MODES = 64
STRIP_LINES = 2097152
LINES = 8192
COLS = 24576
LAG_MIN = 20480
COL_RIM = 9
N_ALONG = 32


def image_draw(key, salt):
    seeded = jax.random.fold_in(key, salt)
    noise_key, row_key, col_key = jax.random.split(seeded, 3)
    noise = jnp.clip(jax.random.normal(noise_key, (LINES, COLS), jnp.float32), -4.0, 4.0)
    row_scale = jnp.exp(jax.random.uniform(row_key, (LINES, 1), jnp.float32, jnp.log(0.3), jnp.log(3.0)))
    col_scale = jnp.exp(jax.random.uniform(col_key, (1, COLS), jnp.float32, jnp.log(0.3), jnp.log(3.0)))
    return (noise * row_scale * col_scale).astype(jnp.bfloat16)


def forced_ints(key, count, lowest, highest):
    values = jax.random.randint(key, (count,), lowest, highest + 1, dtype=jnp.int32)
    order = jax.random.permutation(jax.random.fold_in(key, 7), count)
    values = values.at[order[0]].set(highest)
    return values.at[order[1]].set(lowest)


def draw_nadir_view(key, part):
    return image_draw(key, 11)


def draw_forward(key, part):
    return image_draw(key, 12)


def draw_backward(key, part):
    return image_draw(key, 13)


def draw_lag_lines(key, part):
    seeded = jax.random.fold_in(key, 21)
    values = forced_ints(seeded, LINES, LAG_MIN, LAG_MIN + LAG_SPAN - 1)
    order = jax.random.permutation(jax.random.fold_in(seeded, 9), LINES)
    every = LAG_MIN + jnp.arange(LAG_SPAN, dtype=jnp.int32)
    return values.at[order[2:2 + LAG_SPAN]].set(every)


def draw_band_offsets(key, part):
    return forced_ints(jax.random.fold_in(key, 22), 2 * LINES, -OFFA, OFFA).reshape(2, LINES)


def draw_col_offsets(key, part):
    return forced_ints(jax.random.fold_in(key, 23), 2 * COLS, -OFFC, OFFC).reshape(2, COLS)


def shard_levels(stream_key, dims, cuts, least, top_value):
    gain, own = 1.0, jax.random.fold_in(stream_key, 6)
    for axis_at, shards_of in cuts:
        heights = jnp.exp(jax.random.uniform(jax.random.fold_in(own, axis_at), (shards_of,), jnp.float32, least / len(cuts), top_value / len(cuts)))
        gain = gain * jnp.repeat(heights, dims[axis_at] // shards_of).reshape([-1 if axis == axis_at else 1 for axis in range(len(dims))])
    return gain


def setup_inputs(seed: int = 0) -> dict:
    arg_keys = jax.random.split(jax.random.key(seed), 10)
    nadir_view = draw_nadir_view(jax.random.fold_in(arg_keys[9], 71), 0)
    forward = draw_forward(jax.random.fold_in(arg_keys[9], 71), 0)
    backward = draw_backward(jax.random.fold_in(arg_keys[9], 71), 0)
    along_weights = jnp.clip(jax.random.uniform(arg_keys[3], (2, TAPS, LINES), jnp.float32, 0.049804688, 0.5), 0.049804688, 0.5).astype(jnp.bfloat16)
    cross_weights = jnp.clip(0.049804688 + 0.4501953 * jax.random.uniform(arg_keys[4], (2, TAPS, COLS), jnp.float32) ** shard_levels(arg_keys[4], (2, TAPS, COLS), ((2, 16),), -0.2, 0.2), 0.049804688, 0.5).astype(jnp.bfloat16)
    band_offsets = draw_band_offsets(jax.random.fold_in(arg_keys[9], 71), 0)
    col_offsets = draw_col_offsets(jax.random.fold_in(arg_keys[9], 71), 0)
    lag_lines = draw_lag_lines(jax.random.fold_in(arg_keys[9], 71), 0)
    window_start = jax.random.randint(arg_keys[8], (1,), 0, STRIP_LINES - LINES + 1).astype(jnp.int32)
    return {"nadir_view": nadir_view, "forward": forward, "backward": backward, "along_weights": along_weights, "cross_weights": cross_weights, "band_offsets": band_offsets, "col_offsets": col_offsets, "lag_lines": lag_lines, "window_start": window_start}


def harmonics(absolute):
    period = 4 * MODES
    factor = 2 * jnp.arange(MODES, dtype=jnp.int32) + 1
    phases = ((absolute % period)[:, None] * factor[None, :]) % period
    angles = phases.astype(jnp.float32) * (2.0 * jnp.pi / period)
    return jnp.concatenate([jnp.cos(angles), jnp.sin(angles)], axis=1)


def box_mean(values):
    running = values[0:LD]
    for offset in range(1, 2 * BOX + 1):
        running = running + values[offset:offset + LD]
    return running / (2 * BOX + 1)


def resample_slab(slab, sign, weights_along, offsets_along, weights_cross, offsets_cross, lag_lines, lines_ext):
    wrapped = lines_ext % LINES
    source = lines_ext + sign * jnp.take(lag_lines, wrapped) + jnp.take(offsets_along, wrapped)
    tap_range = jnp.arange(TAPS, dtype=jnp.int32)
    row_index = ((source[:, None] + tap_range[None, :]) % LINES).reshape(-1)
    gathered = jnp.take(slab, row_index, axis=0).reshape(lines_ext.shape[0], TAPS, COLS).astype(jnp.float32)
    tap_weights = jnp.take(weights_along, wrapped, axis=1).T.astype(jnp.float32)
    along = jnp.sum(gathered * tap_weights[:, :, None], axis=1).astype(jnp.bfloat16)
    padded = jnp.pad(along, ((0, 0), (COL_RIM, COL_RIM)))
    columns = jnp.arange(COLS, dtype=jnp.int32)
    result = jnp.zeros((lines_ext.shape[0], COLS), jnp.float32)
    for tap_index in range(TAPS):
        picked = jnp.take(padded, columns + offsets_cross + tap_index + COL_RIM, axis=1)
        result = result + picked.astype(jnp.float32) * weights_cross[tap_index].astype(jnp.float32)[None, :]
    return result.astype(jnp.bfloat16)


def reference(nadir_view, forward, backward, along_weights, cross_weights, band_offsets, col_offsets, lag_lines, window_start):
    columns = jnp.arange(COLS, dtype=jnp.int32)
    position = (columns.astype(jnp.float32) + 0.5) / COLS + 0.25
    lever_two = position * position
    lever_three = lever_two * position
    lever_four = lever_two * lever_two
    scale_sum = 1.0 / (LD * COLS)
    scale_pull = 1.0 / (LD * COLS) ** 0.5

    def one_block(block):
        first_line = block * LD
        lines_ext = first_line + jnp.arange(-BOX, LD + BOX, dtype=jnp.int32)
        lead_res = resample_slab(forward, -1, along_weights[0], band_offsets[0], cross_weights[0], col_offsets[0], lag_lines, lines_ext)
        trail_res = resample_slab(backward, 1, along_weights[1], band_offsets[1], cross_weights[1], col_offsets[1], lag_lines, lines_ext)
        nadir_rows = (first_line + jnp.arange(-BOX - 1, LD + BOX + 1, dtype=jnp.int32)) % LINES
        framed = jnp.pad(jnp.take(nadir_view, nadir_rows, axis=0).astype(jnp.float32), ((0, 0), (1, 1)))
        slopes = (framed[2:, :-2] + 2.0 * framed[2:, 1:-1] + framed[2:, 2:] - framed[:-2, :-2] - 2.0 * framed[:-2, 1:-1] - framed[:-2, 2:]) / 4.0
        center = framed[1:-1, 1:-1]
        texture = box_mean(slopes * slopes)
        divisor = jnp.maximum(texture, 0.4)
        lead_est = -box_mean(slopes * (lead_res.astype(jnp.float32) - center)) / divisor
        trail_est = -box_mean(slopes * (trail_res.astype(jnp.float32) - center)) / divisor
        disagree = lead_est + trail_est
        second = jnp.sum(texture * lever_two[None, :], axis=1) * scale_sum
        third = jnp.sum(texture * lever_three[None, :], axis=1) * scale_sum
        fourth = jnp.sum(texture * lever_four[None, :], axis=1) * scale_sum
        pull_one = jnp.sum(texture * disagree * position[None, :], axis=1) * scale_pull
        pull_two = jnp.sum(texture * disagree * lever_two[None, :], axis=1) * scale_pull
        basis_lines = harmonics(window_start[0] + first_line + jnp.arange(LD, dtype=jnp.int32))

        def weighted(coefs):
            return jnp.dot((basis_lines * coefs[:, None]).T, basis_lines, precision=lax.Precision.HIGHEST)

        gram_block = jnp.concatenate([
            jnp.concatenate([weighted(second), weighted(third)], axis=1),
            jnp.concatenate([weighted(third), weighted(fourth)], axis=1)], axis=0)
        rhs_block = jnp.concatenate([
            jnp.dot(basis_lines.T, pull_one, precision=lax.Precision.HIGHEST),
            jnp.dot(basis_lines.T, pull_two, precision=lax.Precision.HIGHEST)])
        parallax_block = jnp.stack([lead_est, trail_est]).astype(jnp.bfloat16)
        return parallax_block, gram_block, rhs_block

    parallax_all, normal_gram, normal_rhs = lax.map(one_block, jnp.arange(N_ALONG, dtype=jnp.int32))
    parallax = jnp.transpose(parallax_all, (1, 0, 2, 3)).reshape(2, LINES, COLS)
    return parallax, normal_gram, normal_rhs
```

```python
import jax
import jax.numpy as jnp
from jax import lax
from jax.experimental import pallas as pl
from jax.experimental.pallas import tpu as pltpu
from jax.sharding import PartitionSpec as P

TAPS = 4
CAMERA_LAG = 20480
BOX = 4
MODES = 64
LINE_RIM = 32
COL_RIM = 9


def shifted(value, axis, steps):
    count = lax.axis_size(axis)
    pairs = [(source, (source + steps) % count) for source in range(count)]
    return lax.ppermute(value, axis, pairs)


def extended(cells, sides, width):
    for axis, dim in sides:
        count = lax.axis_size(axis)
        ends = count - 1
        head = lax.slice_in_dim(cells, 0, width, axis=dim)
        tail = lax.slice_in_dim(cells, cells.shape[dim] - width, cells.shape[dim], axis=dim)
        cells = jnp.concatenate(
            [
                lax.ppermute(tail, axis, [(i, (i + 1) % count) for i in range(ends)]),
                cells,
                lax.ppermute(head, axis, [((i + 1) % count, i) for i in range(ends)]),
            ],
            axis=dim,
        )
    return cells


def harmonics(absolute):
    period = 4 * MODES
    factor = 2 * jnp.arange(MODES, dtype=jnp.int32) + 1
    phases = (absolute % period)[:, None] * factor[None, :] % period
    angles = phases.astype(jnp.float32) * (2.0 * jnp.pi / period)
    return jnp.concatenate([jnp.cos(angles), jnp.sin(angles)], axis=1)


def box_mean(values, count):
    running = values[0:count]
    for offset in range(1, 2 * BOX + 1):
        running = running + values[offset : offset + count]
    return running / (2 * BOX + 1)


def shift_slabs(lead_part, trail_part, distance):
    lead_moved = shifted(lead_part, "along", distance)
    trail_moved = shifted(trail_part, "along", -distance)
    return (lead_moved, trail_moved)


def line_margin(stacked):
    height = stacked.shape[1]
    from_below = shifted(stacked[:, height - LINE_RIM :], "along", 1)
    from_above = shifted(stacked[:, :LINE_RIM], "along", -1)
    return jnp.concatenate([from_below, stacked, from_above], axis=1)


def column_margin(stacked):
    return extended(stacked, (("cross", 2),), COL_RIM)


def margins(stacked):
    return column_margin(line_margin(stacked))


def sum_kernel(terms_ref, out_ref, gathered, send_sem, recv_sem):
    count = lax.axis_size("cross")
    me = lax.axis_index("cross")
    barrier = pltpu.get_barrier_semaphore()
    for step in range(1, count):
        pl.semaphore_signal(
            barrier,
            inc=1,
            device_id={"cross": lax.rem(me + step, count)},
            device_id_type=pl.DeviceIdType.MESH,
        )
    pl.semaphore_wait(barrier, count - 1)
    copies = []
    for step in range(1, count):
        copies.append(
            pltpu.make_async_remote_copy(
                src_ref=terms_ref,
                dst_ref=gathered.at[step],
                send_sem=send_sem.at[step],
                recv_sem=recv_sem.at[step],
                device_id={"cross": lax.rem(me + step, count)},
                device_id_type=pl.DeviceIdType.MESH,
            )
        )
    for copy in copies:
        copy.start()
    for copy in copies:
        copy.wait()
    total = terms_ref[...]
    for step in range(1, count):
        total = total + gathered[step]
    out_ref[...] = total


def cross_sum(terms):
    count = lax.axis_size("cross")
    return pl.pallas_call(
        sum_kernel,
        out_shape=jax.ShapeDtypeStruct(terms.shape, terms.dtype),
        in_specs=[pl.BlockSpec(memory_space=pltpu.VMEM)],
        out_specs=pl.BlockSpec(memory_space=pltpu.VMEM),
        scratch_shapes=[
            pltpu.VMEM((count,) + terms.shape, terms.dtype),
            pltpu.SemaphoreType.DMA((count,)),
            pltpu.SemaphoreType.DMA((count,)),
        ],
        compiler_params=pltpu.CompilerParams(collective_id=0, has_side_effects=True),
    )(terms)


def along_resample(slab_ext, tap_weights, row_start):
    positions = jnp.arange(slab_ext.shape[0], dtype=jnp.int32)
    distance = positions[None, :] - row_start[:, None]
    banded = jnp.zeros(distance.shape, jnp.bfloat16)
    for tap_index in range(TAPS):
        banded = jnp.where(distance == tap_index, tap_weights[tap_index][:, None], banded)
    return jnp.dot(banded, slab_ext, preferred_element_type=jnp.float32).astype(jnp.bfloat16)


def cross_resample(along_ext, tap_weights, col_shift):
    out_width = col_shift.shape[0]
    tile_count = out_width // 128
    window = 128 + 2 * COL_RIM
    positions = jnp.arange(window, dtype=jnp.int32)
    starts = (
        COL_RIM + jnp.arange(128, dtype=jnp.int32)[None, :] + col_shift.reshape(tile_count, 128)
    )
    distance = positions[None, :, None] - starts[:, None, :]
    banded = jnp.zeros(distance.shape, jnp.bfloat16)
    for tap_index in range(TAPS):
        banded = jnp.where(
            distance == tap_index, tap_weights[tap_index].reshape(tile_count, 1, 128), banded
        )
    pieces = jnp.stack(
        [
            along_ext[:, tile_index * 128 : tile_index * 128 + window]
            for tile_index in range(tile_count)
        ]
    )
    product = jnp.einsum("qla,qaj->lqj", pieces, banded, preferred_element_type=jnp.float32)
    return product.reshape(along_ext.shape[0], out_width).astype(jnp.bfloat16)


def local(
    nadir_view,
    forward,
    backward,
    along_weights,
    cross_weights,
    band_offsets,
    col_offsets,
    lag_lines,
    window_start,
):
    lines_dev, cols_dev = nadir_view.shape
    along_count = lax.axis_size("along")
    cross_count = lax.axis_size("cross")
    along_index = lax.axis_index("along")
    cross_index = lax.axis_index("cross")
    total_lines = lines_dev * along_count
    total_cols = cols_dev * cross_count
    lag_blocks = along_count // 2
    lag_floor = CAMERA_LAG // total_lines * total_lines + lag_blocks * lines_dev
    lead_moved, trail_moved = shift_slabs(forward, backward, lag_blocks)
    widened = margins(jnp.stack([nadir_view, lead_moved, trail_moved]))
    nadir_full, lead_full, trail_full = (widened[0], widened[1], widened[2])
    local_lines = jnp.arange(-BOX, lines_dev + BOX, dtype=jnp.int32)
    wrapped = (along_index * lines_dev + local_lines) % total_lines
    lag_excess = jnp.take(lag_lines, wrapped) - lag_floor
    lead_start = LINE_RIM + local_lines - lag_excess + jnp.take(band_offsets[0], wrapped)
    trail_start = LINE_RIM + local_lines + lag_excess + jnp.take(band_offsets[1], wrapped)
    lead_along = along_resample(lead_full, jnp.take(along_weights[0], wrapped, axis=1), lead_start)
    trail_along = along_resample(
        trail_full, jnp.take(along_weights[1], wrapped, axis=1), trail_start
    )
    lead_res = cross_resample(lead_along, cross_weights[0], col_offsets[0])
    trail_res = cross_resample(trail_along, cross_weights[1], col_offsets[1])
    framed = nadir_full[
        LINE_RIM - BOX - 1 : LINE_RIM + lines_dev + BOX + 1, COL_RIM - 1 : COL_RIM + cols_dev + 1
    ].astype(jnp.float32)
    slopes = (
        framed[2:, :-2]
        + 2.0 * framed[2:, 1:-1]
        + framed[2:, 2:]
        - framed[:-2, :-2]
        - 2.0 * framed[:-2, 1:-1]
        - framed[:-2, 2:]
    ) / 4.0
    center = framed[1:-1, 1:-1]
    texture = box_mean(slopes * slopes, lines_dev)
    divisor = jnp.maximum(texture, 0.4)
    lead_est = -box_mean(slopes * (lead_res.astype(jnp.float32) - center), lines_dev) / divisor
    trail_est = -box_mean(slopes * (trail_res.astype(jnp.float32) - center), lines_dev) / divisor
    parallax = jnp.stack([lead_est, trail_est]).astype(jnp.bfloat16)
    disagree = lead_est + trail_est
    columns = cross_index * cols_dev + jnp.arange(cols_dev, dtype=jnp.int32)
    position = (columns.astype(jnp.float32) + 0.5) / total_cols + 0.25
    lever_two = position * position
    lever_three = lever_two * position
    lever_four = lever_two * lever_two
    scale_sum = 1.0 / (lines_dev * total_cols)
    scale_pull = 1.0 / (lines_dev * total_cols) ** 0.5
    line_terms = jnp.stack(
        [
            jnp.sum(texture * lever_two[None, :], axis=1) * scale_sum,
            jnp.sum(texture * lever_three[None, :], axis=1) * scale_sum,
            jnp.sum(texture * lever_four[None, :], axis=1) * scale_sum,
            jnp.sum(texture * disagree * position[None, :], axis=1) * scale_pull,
            jnp.sum(texture * disagree * lever_two[None, :], axis=1) * scale_pull,
        ]
    )
    basis_lines = harmonics(
        window_start[0] + along_index * lines_dev + jnp.arange(lines_dev, dtype=jnp.int32)
    )

    summed = cross_sum(jnp.concatenate([line_terms, jnp.zeros((3, lines_dev), jnp.float32)]))
    rows_dev = 4 * MODES // cross_count
    half = cross_index // (cross_count // 2)
    first = (cross_index % (cross_count // 2)) * rows_dev
    mine = lax.dynamic_slice_in_dim(basis_lines, first, rows_dev, axis=1)
    weights = lax.dynamic_slice_in_dim(summed, half, 2, axis=0)
    pull = lax.dynamic_slice_in_dim(summed, 3 + half, 1, axis=0)[0]
    scaled = mine[:, None, :] * weights.T[:, :, None]
    gram = jnp.einsum("gqm,gn->mqn", scaled, basis_lines, precision=lax.Precision.HIGHEST)
    normal_gram = gram.reshape(1, rows_dev, 4 * MODES)
    normal_rhs = jnp.sum(mine * pull[:, None], axis=0)[None]
    return (parallax, normal_gram, normal_rhs)


def solution(mesh):
    placed = (
        P("along", "cross"),
        P("along", "cross"),
        P("along", "cross"),
        P(),
        P(None, None, "cross"),
        P(),
        P(None, "cross"),
        P(),
        P(),
    )
    return jax.shard_map(
        local,
        mesh=mesh,
        in_specs=placed,
        out_specs=(P(None, "along", "cross"), P("along", "cross", None), P("along", "cross")),
        check_vma=False,
    )
```
